32 devices in a mesh: ctx: 16 (over z, y, core), head: 2 (over x).
Axes of the slice: x: 2, y: 2, z: 4, core: 2. Of those that a mesh axis runs over, the one named last changes fastest.
Arguments:
- queries: bfloat16 [8192, 2048], P('ctx', 'head'), may hold values from -6 to 6
- keys: bfloat16 [8192, 2048], P('ctx', 'head'), may hold values from -6 to 6
- values: bfloat16 [8192, 2048], P('ctx', 'head'), may hold values from -6 to 6
- rates: float32 [8192, 2], P('ctx', 'head'), may hold values from 0.0005524272 to 0.0055242716
- w_up: bfloat16 [2, 1024, 512], P('head'), may hold values from -0.1875 to 0.1875
- w_gate: bfloat16 [2, 1024, 512], P('head'), may hold values from -0.1875 to 0.1875
- w_down: bfloat16 [2, 512, 1024], P('head'), may hold values from -0.25 to 0.25
- w_out: bfloat16 [2048, 5120], P('head'), may hold values from -0.125 to 0.125
Outputs:
- mixed: bfloat16 [8192, 5120], P('ctx', 'head')
The draws below stay inside these ranges and needn't reach their ends.
All inputs are finite; a program needn't handle non-finite values.
Results may differ from the reference program's by a relative error of at most 0.018.
Values may be sent and summed in bfloat16 or wider, within the bound.
A program may use at most 128 MiB of HBM per device.

```python
import math
import jax
import jax.numpy as jnp
from jax import lax

D = 5120
FD = 1024
FH = 512
STEPS = 2
FHEADS = 2
TOKENS = 8192


def steps_of(own_key, shape, cuts, low, high):
    def one(position, shards_of):
        heights = jax.random.uniform(jax.random.fold_in(jax.random.fold_in(own_key, 6), position), (shards_of,), jnp.float32, low / len(cuts), high / len(cuts))
        return jnp.repeat(jnp.exp(heights), shape[position] // shards_of).reshape((-1,) + (1,) * (len(shape) - position - 1))

    loudness = one(*cuts[0])
    for cut in cuts[1:]:
        loudness = loudness * one(*cut)
    return loudness


def bell_draw(key, shape, spread, limit, cuts=(), held_as=jnp.bfloat16):
    entries = jax.random.normal(key, shape, jnp.float32) * spread
    if len(cuts) > 0:
        entries = steps_of(key, shape, cuts, -0.22, 0.18) * entries
    return jnp.clip(entries, min=-limit, max=limit).astype(held_as)


def setup_inputs(seed: int = 0) -> dict:
    key_of = jax.random.split(jax.random.key(seed), 9)
    return {
        "queries": bell_draw(key_of[0], (TOKENS, FHEADS * FD), 1.0, 6.0, ((0, 16), (1, 2))),
        "keys": bell_draw(key_of[1], (TOKENS, FHEADS * FD), 1.0, 6.0, ((0, 16), (1, 2))),
        "values": bell_draw(key_of[2], (TOKENS, FHEADS * FD), 1.0, 6.0, ((0, 16), (1, 2))),
        "rates": jnp.clip(jnp.exp(math.log(0.0055242716) - 2.30258503 * jax.random.uniform(key_of[3], (TOKENS, FHEADS), jnp.float32) ** steps_of(key_of[3], (TOKENS, FHEADS), ((0, 16), (1, 2)), -0.2, 0.2)), 0.0005524272, 0.0055242716),
        "w_up": bell_draw(key_of[4], (FHEADS, FD, FH), FD ** -0.5, 0.1875, ((0, 2),)),
        "w_gate": bell_draw(key_of[5], (FHEADS, FD, FH), FD ** -0.5, 0.1875, ((0, 2),)),
        "w_down": bell_draw(key_of[6], (FHEADS, FH, FD), FH ** -0.5, 0.25, ((0, 2),)),
        "w_out": bell_draw(key_of[7], (FHEADS * FD, D), (FHEADS * FD) ** -0.5, 0.125, ((0, 2),)),
    }


def frob(matrix):
    return jnp.sqrt(jnp.sum(matrix * matrix))

def tdot(left, right):
    return lax.dot_general(left, right, (((0,), (0,)), ((), ())), preferred_element_type=jnp.float32)

def one_head(keys_h, values_h, queries_h, rate, first, third, second):
    sizes = [frob(first), frob(third), frob(second)]
    targets = (rate[:, None] * values_h.astype(jnp.float32)).astype(jnp.bfloat16)
    weights = [first, third, second]
    for step in range(STEPS):
        b_one = weights[0].astype(jnp.bfloat16)
        b_three = weights[1].astype(jnp.bfloat16)
        b_two = weights[2].astype(jnp.bfloat16)
        act = jnp.dot(keys_h, b_one, preferred_element_type=jnp.float32)
        lin = jnp.dot(keys_h, b_three, preferred_element_type=jnp.float32)
        sig = jax.nn.sigmoid(act)
        hidden = (act * sig * lin).astype(jnp.bfloat16)
        err = lax.dot_general(targets, b_two, (((1,), (1,)), ((), ())), preferred_element_type=jnp.float32)
        pgrad = (err * lin * sig * (1.0 + act * (1.0 - sig))).astype(jnp.bfloat16)
        qgrad = (err * act * sig).astype(jnp.bfloat16)
        grads = [tdot(keys_h, pgrad), tdot(keys_h, qgrad), tdot(hidden, targets)]
        updated = []
        for weight, grad, size in zip(weights, grads, sizes):
            moved = weight + grad
            updated.append(moved * size / jnp.sqrt(jnp.sum(moved * moved) + 1e-06))
        weights = updated
    b_one = weights[0].astype(jnp.bfloat16)
    b_three = weights[1].astype(jnp.bfloat16)
    b_two = weights[2].astype(jnp.bfloat16)
    act = jnp.dot(queries_h, b_one, preferred_element_type=jnp.float32)
    lin = jnp.dot(queries_h, b_three, preferred_element_type=jnp.float32)
    hidq = (jax.nn.silu(act) * lin).astype(jnp.bfloat16)
    return jnp.dot(hidq, b_two, preferred_element_type=jnp.float32).astype(jnp.bfloat16)

def reference(queries, keys, values, rates, w_up, w_gate, w_down, w_out):
    pieces = []
    for head in range(FHEADS):
        lo = head * FD
        pieces.append(one_head(keys[:, lo:lo + FD], values[:, lo:lo + FD], queries[:, lo:lo + FD], rates[:, head], w_up[head].astype(jnp.float32), w_gate[head].astype(jnp.float32), w_down[head].astype(jnp.float32)))
    joined = jnp.concatenate(pieces, axis=1)
    return jnp.dot(joined, w_out, preferred_element_type=jnp.float32).astype(jnp.bfloat16)
```

```python
import jax
import jax.numpy as jnp
from jax import lax
from jax.sharding import PartitionSpec as P

STEPS = 2
F32 = jnp.float32
BF16 = jnp.bfloat16


def dot(left, right, dims=((1,), (0,))):
    return lax.dot_general(left, right, (dims, ((), ())), preferred_element_type=F32)


def shards(n_ctx, queries, keys, values, rates, w_up, w_gate, w_down, w_out):
    head = lax.axis_index("head")
    half = w_out.shape[1] // 2
    swap = [(0, 1), (1, 0)]
    w_near = lax.dynamic_slice_in_dim(w_out, head * half, half, 1)
    w_far = lax.ppermute(
        lax.dynamic_slice_in_dim(w_out, (1 - head) * half, half, 1), "head", swap
    )
    targets = (rates[:, 0][:, None] * values.astype(F32)).astype(BF16)
    blocks = jnp.stack([w_up[0], w_gate[0], w_down[0].T])
    sizes = jnp.sqrt(jnp.sum(blocks.astype(F32) ** 2, axis=(1, 2)))
    scales = jnp.ones((3,), F32)
    depth = blocks.shape[1] // n_ctx
    mine = lax.dynamic_slice_in_dim(
        blocks, lax.axis_index("ctx") * depth, depth, 1
    ).astype(F32)
    for step in range(STEPS):
        act = scales[0] * dot(keys, blocks[0])
        lin = scales[1] * dot(keys, blocks[1])
        err = scales[2] * dot(targets, blocks[2])
        sig = jax.nn.sigmoid(act)
        hidden = (act * sig * lin).astype(BF16)
        pgrad = (err * lin * sig * (1.0 + act * (1.0 - sig))).astype(BF16)
        qgrad = (err * act * sig).astype(BF16)
        rows = ((0,), (0,))
        grads = jnp.stack(
            [
                dot(keys, pgrad, rows).astype(BF16),
                dot(keys, qgrad, rows).astype(BF16),
                dot(targets, hidden, rows).astype(BF16),
            ]
        )
        total = lax.psum_scatter(grads, "ctx", scatter_dimension=1, tiled=True)
        moved = mine * scales[:, None, None] + total.astype(F32)
        mine = moved
        blocks = lax.all_gather(moved.astype(BF16), "ctx", axis=1, tiled=True)
        scales = sizes / jnp.sqrt(jnp.sum(blocks.astype(F32) ** 2, axis=(1, 2)) + 1e-06)
    act = scales[0] * dot(queries, blocks[0])
    lin = scales[1] * dot(queries, blocks[1])
    hidq = (jax.nn.silu(act) * lin).astype(BF16)
    near = (scales[2] * dot(hidq, blocks[2], ((1,), (1,)))).astype(BF16)
    far = lax.ppermute(near, "head", swap)
    return (dot(near, w_near) + dot(far, w_far)).astype(BF16)


def solution(mesh):
    def body(*args):
        return shards(mesh.shape["ctx"], *args)

    return jax.shard_map(
        body,
        mesh=mesh,
        in_specs=(
            P("ctx", "head"),
            P("ctx", "head"),
            P("ctx", "head"),
            P("ctx", "head"),
            P("head", None, None),
            P("head", None, None),
            P("head", None, None),
            P("head", None),
        ),
        out_specs=P("ctx", "head"),
        check_vma=False,
    )
```

```python
import functools

import jax
import jax.numpy as jnp
from jax import lax
from jax.experimental import pallas as pl
from jax.experimental.pallas import tpu as pltpu
from jax.sharding import PartitionSpec as P

STEPS = 2
F32 = jnp.float32
BF16 = jnp.bfloat16
MESH = pl.DeviceIdType.MESH
GROUP = 3


def orders_of(n_ctx):
    bits = list(range(n_ctx.bit_length() - 1))
    return [bits, bits[:1] + bits[2:] + bits[1:2]]


def bit_of(me, bit):
    return (me // (1 << bit)) % 2


def start_of(me, order, rows):
    start = 0
    for bit in order:
        rows = rows // 2
        start = start + bit_of(me, bit) * rows
    return start


def lanes_of(part, cols):
    width = cols // 2
    return slice(part * width, (part + 1) * width)


def exchange_kernel(n_ctx, g0, g1, g2, mine, o0, o1, o2, kept, sums, *scratch):
    grads, outs = (g0, g1, g2), (o0, o1, o2)
    rows, cols = g0.shape
    orders = orders_of(n_ctx)
    count = len(orders[0])
    recvs = scratch[:count]
    accs = scratch[count : 2 * count - 1]
    send_sem, recv_sem = scratch[2 * count - 1 :]
    me = lax.axis_index("ctx")

    def partner_of(bit):
        return me + (1 - 2 * bit_of(me, bit)) * (1 << bit)

    barrier = pltpu.get_barrier_semaphore()
    for bit in range(count):
        pl.semaphore_signal(
            barrier, inc=1, device_id={"ctx": partner_of(bit)}, device_id_type=MESH
        )
    pl.semaphore_wait(barrier, count)

    chains = [(w, part) for part in range(2) for w in range(GROUP)]
    copies = {}

    def send(chain, slot, source, target, bit):
        copy = pltpu.make_async_remote_copy(
            src_ref=source,
            dst_ref=target,
            send_sem=send_sem.at[chain, slot],
            recv_sem=recv_sem.at[chain, slot],
            device_id={"ctx": partner_of(bit)},
            device_id_type=MESH,
        )
        copy.start()
        copies[chain, slot] = copy

    def send_down(chain, stage):
        w, part = chains[chain]
        lanes = lanes_of(part, cols)
        bit = orders[part][stage]
        size = rows >> (stage + 1)
        away = pl.ds(pl.multiple_of((1 - bit_of(me, bit)) * size, size), size)
        if stage == 0:
            source = grads[w].at[away, lanes]
        else:
            source = accs[stage - 1].at[w, away, lanes]
        send(chain, stage, source, recvs[stage].at[w, :, lanes], bit)

    def region(chain, stage):
        w, part = chains[chain]
        size = rows >> stage
        start = start_of(me, orders[part][:stage], rows)
        return pl.ds(pl.multiple_of(start, size), size)

    def send_up(chain, stage):
        w, part = chains[chain]
        lanes = lanes_of(part, cols)
        place = outs[w].at[region(chain, stage + 1), lanes]
        send(chain, 2 * count - 1 - stage, place, place, orders[part][stage])

    def square_sum(block):
        return jnp.sum((block * block).reshape(-1, 8, block.shape[-1]), axis=0)

    for chain in range(len(chains)):
        send_down(chain, 0)
    for stage in range(count):
        size = rows >> (stage + 1)
        for chain, (w, part) in enumerate(chains):
            lanes = lanes_of(part, cols)
            bit = orders[part][stage]
            near = pl.ds(pl.multiple_of(bit_of(me, bit) * size, size), size)
            copies[chain, stage].wait_recv()
            held = grads[w][near, lanes] if stage == 0 else accs[stage - 1][w, near, lanes]
            total = held.astype(F32) + recvs[stage][w, :, lanes].astype(F32)
            if stage < count - 1:
                accs[stage][w, :, lanes] = total.astype(BF16)
                send_down(chain, stage + 1)
            else:
                moved = mine[part, w] + total
                kept[part, w] = moved
                rounded = moved.astype(BF16)
                outs[w][region(chain, count), lanes] = rounded
                send_up(chain, count - 1)
                sums[w, :, lanes] = square_sum(rounded.astype(F32))
    for stage in reversed(range(count)):
        size = rows >> (stage + 1)
        for chain, (w, part) in enumerate(chains):
            lanes = lanes_of(part, cols)
            copies[chain, 2 * count - 1 - stage].wait_recv()
            if stage > 0:
                send_up(chain, stage - 1)
            bit = orders[part][stage]
            other = start_of(me, orders[part][:stage], rows)
            other = other + (1 - bit_of(me, bit)) * size
            place = pl.ds(pl.multiple_of(other, size), size)
            sums[w, :, lanes] += square_sum(outs[w][place, lanes].astype(F32))
    for copy in copies.values():
        copy.wait_send()


def exchange(n_ctx, grads, mine):
    rows, cols = grads[0].shape
    count = n_ctx.bit_length() - 1
    full = jax.ShapeDtypeStruct((rows, cols), BF16)
    chains = 2 * GROUP
    sent = 2 * GROUP * rows * cols * 2
    return pl.pallas_call(
        functools.partial(exchange_kernel, n_ctx),
        out_shape=[
            full,
            full,
            full,
            jax.ShapeDtypeStruct(mine.shape, F32),
            jax.ShapeDtypeStruct((GROUP, 8, cols), F32),
        ],
        in_specs=[pl.BlockSpec(memory_space=pltpu.VMEM)] * 4,
        out_specs=[pl.BlockSpec(memory_space=pltpu.VMEM)] * 5,
        scratch_shapes=[
            pltpu.VMEM((GROUP, rows >> (stage + 1), cols), BF16)
            for stage in range(count)
        ]
        + [
            pltpu.VMEM((GROUP, rows >> (stage + 1), cols), BF16)
            for stage in range(count - 1)
        ]
        + [
            pltpu.SemaphoreType.DMA((chains, 2 * count)),
            pltpu.SemaphoreType.DMA((chains, 2 * count)),
        ],
        compiler_params=pltpu.CompilerParams(
            collective_id=0, has_side_effects=True, vmem_limit_bytes=32 << 20
        ),
        cost_estimate=pl.CostEstimate(
            flops=50_000_000, bytes_accessed=sent * 8, transcendentals=0
        ),
    )(*grads, mine)


def dot(left, right, dims=((1,), (0,))):
    return lax.dot_general(left, right, (dims, ((), ())), preferred_element_type=F32)


def shards(n_ctx, queries, keys, values, rates, w_up, w_gate, w_down, w_out):
    head = lax.axis_index("head")
    me = lax.axis_index("ctx")
    half = w_out.shape[1] // 2
    swap = [(0, 1), (1, 0)]
    w_near = lax.dynamic_slice_in_dim(w_out, head * half, half, 1)
    w_far = lax.ppermute(
        lax.dynamic_slice_in_dim(w_out, (1 - head) * half, half, 1), "head", swap
    )
    targets = (rates[:, 0][:, None] * values.astype(F32)).astype(BF16)
    blocks = [w_up[0], w_gate[0], w_down[0].T]
    rows, cols = blocks[0].shape
    sizes = jnp.stack([jnp.sqrt(jnp.sum(b.astype(F32) ** 2)) for b in blocks])
    scales = jnp.ones((GROUP,), F32)
    mine = jnp.stack(
        [
            jnp.stack(
                [
                    lax.dynamic_slice_in_dim(
                        b[:, lanes_of(part, cols)],
                        start_of(me, order, rows),
                        rows // n_ctx,
                        0,
                    )
                    for b in blocks
                ]
            )
            for part, order in enumerate(orders_of(n_ctx))
        ]
    ).astype(F32)
    for step in range(STEPS):
        act = scales[0] * dot(keys, blocks[0])
        lin = scales[1] * dot(keys, blocks[1])
        err = scales[2] * dot(targets, blocks[2])
        sig = jax.nn.sigmoid(act)
        hidden = (act * sig * lin).astype(BF16)
        pgrad = (err * lin * sig * (1.0 + act * (1.0 - sig))).astype(BF16)
        qgrad = (err * act * sig).astype(BF16)
        over = ((0,), (0,))
        grads = [
            dot(keys, pgrad, over).astype(BF16),
            dot(keys, qgrad, over).astype(BF16),
            dot(targets, hidden, over).astype(BF16),
        ]
        *blocks, mine, sums = exchange(n_ctx, grads, mine * scales[:, None, None])
        scales = sizes / jnp.sqrt(jnp.sum(sums, axis=(1, 2)) + 1e-06)
    act = scales[0] * dot(queries, blocks[0])
    lin = scales[1] * dot(queries, blocks[1])
    hidq = (jax.nn.silu(act) * lin).astype(BF16)
    near = (scales[2] * dot(hidq, blocks[2], ((1,), (1,)))).astype(BF16)
    far = lax.ppermute(near, "head", swap)
    return (dot(near, w_near) + dot(far, w_far)).astype(BF16)


def solution(mesh):
    def body(*args):
        return shards(mesh.shape["ctx"], *args)

    return jax.shard_map(
        body,
        mesh=mesh,
        in_specs=(
            P("ctx", "head"),
            P("ctx", "head"),
            P("ctx", "head"),
            P("ctx", "head"),
            P("head", None, None),
            P("head", None, None),
            P("head", None, None),
            P("head", None),
        ),
        out_specs=P("ctx", "head"),
        check_vma=False,
    )
```

```python
import functools

import jax
import jax.numpy as jnp
from jax import lax
from jax.experimental import pallas as pl
from jax.experimental.pallas import tpu as pltpu
from jax.sharding import PartitionSpec as P

STEPS = 2
F32 = jnp.float32
BF16 = jnp.bfloat16
MESH = pl.DeviceIdType.MESH
GROUP = 3


PARTS = 4


def orders_of(n_ctx):
    count = n_ctx.bit_length() - 1
    middle, low, high = list(range(1, count - 2)), count - 2, count - 1
    return [
        [0] + middle + [low, high],
        [0] + middle + [high, low],
        [0, low, high] + middle,
        [0, high, low] + middle,
    ]


def raw_bit(me, bit):
    return (me // (1 << bit)) % 2


def half_of(me, stage, count):
    if stage == count - 2:
        return (raw_bit(me, count - 2) + raw_bit(me, count - 1)) % 2
    return raw_bit(me, stage)


def partner_of(me, stage, count):
    flips = (count - 2, count - 1) if stage == count - 1 else (stage,)
    for bit in flips:
        me = me + (1 - 2 * raw_bit(me, bit)) * (1 << bit)
    return me


def lanes_of(part, cols):
    width = cols // PARTS
    return slice(part * width, (part + 1) * width)


def dot(left, right, dims=((1,), (0,))):
    return lax.dot_general(left, right, (dims, ((), ())), preferred_element_type=F32)


def square_sum(block):
    return jnp.sum((block * block).reshape(-1, 8, block.shape[-1]), axis=0)


def layer_kernel(
    n_ctx, q, k, v, r, w0, w1, w2, w_out, out, *scratch
):
    count = n_ctx.bit_length() - 1
    recvs, scratch = scratch[:count], scratch[count:]
    accs, scratch = scratch[: count - 1], scratch[count - 1 :]
    (
        kt, u, ut, first2, grads, blocks, mid, kept, sums,
        w_near, w_far, near, far, total_out,
        send_sem, recv_sem, swap_send, swap_recv, local_sem,
    ) = scratch
    tokens, rows = k.shape
    cols = w0.shape[1]
    half = w_out.shape[1] // 2
    orders = orders_of(n_ctx)
    me = lax.axis_index("ctx")
    head = lax.axis_index("head")

    def bit_of(stage):
        return half_of(me, stage, count)

    def partner(stage):
        return {"ctx": partner_of(me, stage, count)}

    def start_of(order):
        start, left = 0, rows
        for stage in order:
            left = left // 2
            start = start + bit_of(stage) * left
        return start

    across = {"head": 1 - head}
    barrier = pltpu.get_barrier_semaphore()
    for target in [partner(stage) for stage in range(count)] + [across]:
        pl.semaphore_signal(barrier, inc=1, device_id=target, device_id_type=MESH)
    pl.semaphore_wait(barrier, count + 1)

    def swap(slot, source, target):
        return pltpu.make_async_remote_copy(
            src_ref=source,
            dst_ref=target,
            send_sem=swap_send.at[slot],
            recv_sem=swap_recv.at[slot],
            device_id=across,
            device_id_type=MESH,
        )

    near_cols = pl.ds(pl.multiple_of(head * half, 128), half)
    far_cols = pl.ds(pl.multiple_of((1 - head) * half, 128), half)
    w_swap = swap(0, w_out.at[:, far_cols], w_far)
    w_swap.start()
    w_copy = pltpu.make_async_copy(w_out.at[:, near_cols], w_near, local_sem)
    w_copy.start()

    tile = tokens // 4
    for t in range(4):
        at = slice(t * tile, (t + 1) * tile)
        scaled = (r[at, :] * v[at, :].astype(F32)).astype(BF16)
        u[at, :] = scaled
        ut[:, at] = scaled.T
        kt[:, at] = k[at, :].T
    for t in range(cols // 128):
        at = slice(t * 128, (t + 1) * 128)
        first2[:, at] = w2[at, :].T

    chains = [(w, part) for w in range(GROUP) for part in range(PARTS)]
    firsts = (w0, w1, first2)
    scales = [None] * GROUP
    for step in range(STEPS):
        now = firsts if step == 0 else [blocks.at[w] for w in range(GROUP)]
        copies = {}

        def scaled_dot(w, left):
            product = dot(left, now[w][...])
            return product if scales[w] is None else product * scales[w]

        for t in range(2):
            at = slice(t * (tokens // 2), (t + 1) * (tokens // 2))
            act = scaled_dot(0, k[at, :])
            lin = scaled_dot(1, k[at, :])
            err = scaled_dot(2, u[at, :])
            sig = jax.nn.sigmoid(act)
            gate = act * sig
            mid[0, at, :] = (err * lin * sig * (1.0 + act * (1.0 - sig))).astype(BF16)
            mid[1, at, :] = (err * gate).astype(BF16)
            mid[2, at, :] = (gate * lin).astype(BF16)

        def send(chain, slot, source, target, bit):
            copy = pltpu.make_async_remote_copy(
                src_ref=source,
                dst_ref=target,
                send_sem=send_sem.at[chain, slot],
                recv_sem=recv_sem.at[chain, slot],
                device_id=partner(bit),
                device_id_type=MESH,
            )
            copy.start()
            copies[chain, slot] = copy

        def send_down(chain, stage):
            w, part = chains[chain]
            lanes = lanes_of(part, cols)
            bit = orders[part][stage]
            size = rows >> (stage + 1)
            away = pl.ds(pl.multiple_of((1 - bit_of(bit)) * size, size), size)
            origin = grads if stage == 0 else accs[stage - 1]
            source = origin.at[w, away, lanes]
            send(chain, stage, source, recvs[stage].at[w, :, lanes], bit)

        def region(chain, stage):
            w, part = chains[chain]
            size = rows >> stage
            start = start_of(orders[part][:stage])
            return pl.ds(pl.multiple_of(start, size), size)

        def send_up(chain, stage):
            w, part = chains[chain]
            place = blocks.at[w, region(chain, stage + 1), lanes_of(part, cols)]
            send(chain, 2 * count - 1 - stage, place, place, orders[part][stage])

        for w in range(GROUP):
            left = ut if w == 2 else kt

            def grad_rows(piece, carry):
                at = pl.ds(pl.multiple_of(piece * (rows // 4), rows // 4), rows // 4)
                grads[w, at, :] = dot(left[at, :], mid[w]).astype(BF16)
                return carry

            lax.fori_loop(0, 4, grad_rows, 0)
            for part in range(PARTS):
                send_down(PARTS * w + part, 0)
        if step == 0:
            norms = [
                jnp.sqrt(jnp.sum(square_sum(b[...].astype(F32)), keepdims=True))
                for b in firsts
            ]
        for stage in range(count):
            size = rows >> (stage + 1)
            for chain, (w, part) in enumerate(chains):
                lanes = lanes_of(part, cols)
                bit = orders[part][stage]
                close = pl.ds(pl.multiple_of(bit_of(bit) * size, size), size)
                copies[chain, stage].wait_recv()
                origin = grads if stage == 0 else accs[stage - 1]
                held = origin[w, close, lanes].astype(F32)
                total = held + recvs[stage][w, :, lanes].astype(F32)
                if stage < count - 1:
                    accs[stage][w, :, lanes] = total.astype(BF16)
                    send_down(chain, stage + 1)
                else:
                    place = region(chain, count)
                    if step == 0:
                        moved = firsts[w][place, lanes].astype(F32) + total
                    else:
                        moved = kept[w, :, lanes] * scales[w] + total
                    kept[w, :, lanes] = moved
                    rounded = moved.astype(BF16)
                    blocks[w, place, lanes] = rounded
                    send_up(chain, count - 1)
                    sums[w, :, lanes] = square_sum(rounded.astype(F32))
        for stage in reversed(range(count)):
            size = rows >> (stage + 1)
            for chain, (w, part) in enumerate(chains):
                lanes = lanes_of(part, cols)
                copies[chain, 2 * count - 1 - stage].wait_recv()
                if stage > 0:
                    send_up(chain, stage - 1)
                other = start_of(orders[part][:stage])
                other = other + (1 - bit_of(orders[part][stage])) * size
                place = pl.ds(pl.multiple_of(other, size), size)
                sums[w, :, lanes] += square_sum(blocks[w, place, lanes].astype(F32))
        for copy in copies.values():
            copy.wait_send()
        scales = [
            norms[w] / jnp.sqrt(jnp.sum(sums[w], keepdims=True) + 1e-06)
            for w in range(GROUP)
        ]

    o_swaps = []
    for t in range(4):
        at = slice(t * tile, (t + 1) * tile)
        act = dot(q[at, :], blocks[0]) * scales[0]
        lin = dot(q[at, :], blocks[1]) * scales[1]
        hidq = (act * jax.nn.sigmoid(act) * lin).astype(BF16)
        piece = dot(hidq, blocks[2], ((1,), (1,))) * scales[2]
        near[at, :] = piece.astype(BF16)
        o_swap = swap(1 + t, near.at[at, :], far.at[at, :])
        o_swap.start()
        o_swaps.append(o_swap)
    w_copy.wait()
    width = half // 5

    def near_cols_of(c, carry):
        lanes = pl.ds(pl.multiple_of(c * width, 128), width)
        total_out[:, lanes] = dot(near[...], w_near[:, lanes])
        return carry

    lax.fori_loop(0, 5, near_cols_of, 0)
    w_swap.wait()
    for t in range(4):
        at = slice(t * tile, (t + 1) * tile)
        o_swaps[t].wait_recv()

        def far_cols_of(c, carry):
            lanes = pl.ds(pl.multiple_of(c * width, 128), width)
            added = total_out[at, lanes] + dot(far[at, :], w_far[:, lanes])
            out[at, lanes] = added.astype(BF16)
            return carry

        lax.fori_loop(0, 5, far_cols_of, 0)
    for o_swap in o_swaps:
        o_swap.wait_send()


def shards(n_ctx, queries, keys, values, rates, w_up, w_gate, w_down, w_out):
    tokens, rows = keys.shape
    cols = w_up.shape[2]
    half = w_out.shape[1] // 2
    count = n_ctx.bit_length() - 1
    chains = PARTS * GROUP
    vmem = pl.BlockSpec(memory_space=pltpu.VMEM)
    return pl.pallas_call(
        functools.partial(layer_kernel, n_ctx),
        out_shape=jax.ShapeDtypeStruct((tokens, half), BF16),
        in_specs=[vmem] * 7 + [pl.BlockSpec(memory_space=pl.ANY)],
        out_specs=vmem,
        scratch_shapes=[
            pltpu.VMEM((GROUP, rows >> (stage + 1), cols), BF16)
            for stage in range(count)
        ]
        + [
            pltpu.VMEM((GROUP, rows >> (stage + 1), cols), BF16)
            for stage in range(count - 1)
        ]
        + [
            pltpu.VMEM((rows, tokens), BF16),
            pltpu.VMEM((tokens, rows), BF16),
            pltpu.VMEM((rows, tokens), BF16),
            pltpu.VMEM((rows, cols), BF16),
            pltpu.VMEM((GROUP, rows, cols), BF16),
            pltpu.VMEM((GROUP, rows, cols), BF16),
            pltpu.VMEM((GROUP, tokens, cols), BF16),
            pltpu.VMEM((GROUP, rows // n_ctx, cols), F32),
            pltpu.VMEM((GROUP, 8, cols), F32),
            pltpu.VMEM((rows, half), BF16),
            pltpu.VMEM((rows, half), BF16),
            pltpu.VMEM((tokens, rows), BF16),
            pltpu.VMEM((tokens, rows), BF16),
            pltpu.VMEM((tokens, half), F32),
            pltpu.SemaphoreType.DMA((chains, 2 * count)),
            pltpu.SemaphoreType.DMA((chains, 2 * count)),
            pltpu.SemaphoreType.DMA((5,)),
            pltpu.SemaphoreType.DMA((5,)),
            pltpu.SemaphoreType.DMA,
        ],
        compiler_params=pltpu.CompilerParams(
            collective_id=0, has_side_effects=True, vmem_limit_bytes=60 << 20
        ),
    )(queries, keys, values, rates, w_up[0], w_gate[0], w_down[0], w_out)


def solution(mesh):
    def body(*args):
        return shards(mesh.shape["ctx"], *args)

    return jax.shard_map(
        body,
        mesh=mesh,
        in_specs=(
            P("ctx", "head"),
            P("ctx", "head"),
            P("ctx", "head"),
            P("ctx", "head"),
            P("head", None, None),
            P("head", None, None),
            P("head", None, None),
            P("head", None),
        ),
        out_specs=P("ctx", "head"),
        check_vma=False,
    )
```

```python
import functools

import jax
import jax.numpy as jnp
from jax import lax
from jax.experimental import pallas as pl
from jax.experimental.pallas import tpu as pltpu
from jax.sharding import PartitionSpec as P

STEPS = 2
F32 = jnp.float32
BF16 = jnp.bfloat16
MESH = pl.DeviceIdType.MESH
GROUP = 3


PARTS = 4


def orders_of(n_ctx):
    count = n_ctx.bit_length() - 1
    middle, low, high = list(range(1, count - 2)), count - 2, count - 1
    return [
        [0] + middle + [low, high],
        [0] + middle + [high, low],
        [0, low, high] + middle,
        [0, high, low] + middle,
    ]


def raw_bit(me, bit):
    return (me // (1 << bit)) % 2


def half_of(me, stage, count):
    if stage == count - 2:
        return (raw_bit(me, count - 2) + raw_bit(me, count - 1)) % 2
    return raw_bit(me, stage)


def partner_of(me, stage, count):
    flips = (count - 2, count - 1) if stage == count - 1 else (stage,)
    for bit in flips:
        me = me + (1 - 2 * raw_bit(me, bit)) * (1 << bit)
    return me


def lanes_of(part, cols):
    width = cols // PARTS
    return slice(part * width, (part + 1) * width)


def dot(left, right, dims=((1,), (0,))):
    return lax.dot_general(left, right, (dims, ((), ())), preferred_element_type=F32)


def square_sum(block):
    return jnp.sum((block * block).reshape(-1, 8, block.shape[-1]), axis=0)


def layer_kernel(
    n_ctx, q, k, v, r, w0, w1, w2, w_out, out, *scratch
):
    count = n_ctx.bit_length() - 1
    recvs, scratch = scratch[:count], scratch[count:]
    accs, scratch = scratch[: count - 1], scratch[count - 1 :]
    (
        kt, u, ut, first2, grads, blocks, mid, kept, sums,
        w_near, w_far, near, far, total_out,
        send_sem, recv_sem, swap_send, swap_recv, share_sem, local_sem,
    ) = scratch
    tokens, rows = k.shape
    cols = w0.shape[1]
    half = w_out.shape[1] // 2
    orders = orders_of(n_ctx)
    me = lax.axis_index("ctx")
    head = lax.axis_index("head")

    def bit_of(stage):
        return half_of(me, stage, count)

    def partner(stage):
        return {"ctx": partner_of(me, stage, count)}

    def start_of(order):
        start, left = 0, rows
        for stage in order:
            left = left // 2
            start = start + bit_of(stage) * left
        return start

    across = {"head": 1 - head}
    barrier = pltpu.get_barrier_semaphore()
    for target in [partner(stage) for stage in range(count)] + [across]:
        pl.semaphore_signal(barrier, inc=1, device_id=target, device_id_type=MESH)
    pl.semaphore_wait(barrier, count + 1)

    def swap(slot, source, target):
        return pltpu.make_async_remote_copy(
            src_ref=source,
            dst_ref=target,
            send_sem=swap_send.at[slot],
            recv_sem=swap_recv.at[slot],
            device_id=across,
            device_id_type=MESH,
        )

    near_cols = pl.ds(pl.multiple_of(head * half, 128), half)
    far_cols = pl.ds(pl.multiple_of((1 - head) * half, 128), half)
    depth = rows // 2
    own_rows = pl.ds(pl.multiple_of(raw_bit(me, 0) * depth, depth), depth)
    w_swap = swap(0, w_out.at[own_rows, far_cols], w_far.at[own_rows, :])
    w_swap.start()
    w_copy = pltpu.make_async_copy(w_out.at[:, near_cols], w_near, local_sem)
    w_copy.start()

    tile = tokens // 4
    for t in range(4):
        at = slice(t * tile, (t + 1) * tile)
        scaled = (r[at, :] * v[at, :].astype(F32)).astype(BF16)
        u[at, :] = scaled
        ut[:, at] = scaled.T
        kt[:, at] = k[at, :].T
    for t in range(cols // 128):
        at = slice(t * 128, (t + 1) * 128)
        first2[:, at] = w2[at, :].T

    chains = [(w, part) for w in range(GROUP) for part in range(PARTS)]
    firsts = (w0, w1, first2)
    scales = [None] * GROUP
    for step in range(STEPS):
        now = firsts if step == 0 else [blocks.at[w] for w in range(GROUP)]
        copies = {}

        def scaled_dot(w, left):
            product = dot(left, now[w][...])
            return product if scales[w] is None else product * scales[w]

        for t in range(2):
            at = slice(t * (tokens // 2), (t + 1) * (tokens // 2))
            act = scaled_dot(0, k[at, :])
            lin = scaled_dot(1, k[at, :])
            err = scaled_dot(2, u[at, :])
            sig = jax.nn.sigmoid(act)
            gate = act * sig
            mid[0, at, :] = (err * lin * sig * (1.0 + act * (1.0 - sig))).astype(BF16)
            mid[1, at, :] = (err * gate).astype(BF16)
            mid[2, at, :] = (gate * lin).astype(BF16)

        def send(chain, slot, source, target, bit):
            copy = pltpu.make_async_remote_copy(
                src_ref=source,
                dst_ref=target,
                send_sem=send_sem.at[chain, slot],
                recv_sem=recv_sem.at[chain, slot],
                device_id=partner(bit),
                device_id_type=MESH,
            )
            copy.start()
            copies[chain, slot] = copy

        def send_down(chain, stage):
            w, part = chains[chain]
            lanes = lanes_of(part, cols)
            bit = orders[part][stage]
            size = rows >> (stage + 1)
            away = pl.ds(pl.multiple_of((1 - bit_of(bit)) * size, size), size)
            origin = grads if stage == 0 else accs[stage - 1]
            source = origin.at[w, away, lanes]
            send(chain, stage, source, recvs[stage].at[w, :, lanes], bit)

        def region(chain, stage):
            w, part = chains[chain]
            size = rows >> stage
            start = start_of(orders[part][:stage])
            return pl.ds(pl.multiple_of(start, size), size)

        def send_up(chain, stage):
            w, part = chains[chain]
            place = blocks.at[w, region(chain, stage + 1), lanes_of(part, cols)]
            send(chain, 2 * count - 1 - stage, place, place, orders[part][stage])

        for w in range(GROUP):
            left = ut if w == 2 else kt

            def grad_rows(piece, carry):
                at = pl.ds(pl.multiple_of(piece * (rows // 4), rows // 4), rows // 4)
                grads[w, at, :] = dot(left[at, :], mid[w]).astype(BF16)
                return carry

            lax.fori_loop(0, 4, grad_rows, 0)
            for part in range(PARTS):
                send_down(PARTS * w + part, 0)
        if step == 0:
            norms = [
                jnp.sqrt(jnp.sum(square_sum(b[...].astype(F32)), keepdims=True))
                for b in firsts
            ]
        for stage in range(count):
            size = rows >> (stage + 1)
            for chain, (w, part) in enumerate(chains):
                lanes = lanes_of(part, cols)
                bit = orders[part][stage]
                close = pl.ds(pl.multiple_of(bit_of(bit) * size, size), size)
                copies[chain, stage].wait_recv()
                origin = grads if stage == 0 else accs[stage - 1]
                held = origin[w, close, lanes].astype(F32)
                total = held + recvs[stage][w, :, lanes].astype(F32)
                if stage < count - 1:
                    accs[stage][w, :, lanes] = total.astype(BF16)
                    send_down(chain, stage + 1)
                else:
                    place = region(chain, count)
                    if step == 0:
                        moved = firsts[w][place, lanes].astype(F32) + total
                    else:
                        moved = kept[w, :, lanes] * scales[w] + total
                    kept[w, :, lanes] = moved
                    rounded = moved.astype(BF16)
                    blocks[w, place, lanes] = rounded
                    send_up(chain, count - 1)
                    sums[w, :, lanes] = square_sum(rounded.astype(F32))
        for stage in reversed(range(count)):
            size = rows >> (stage + 1)
            for chain, (w, part) in enumerate(chains):
                lanes = lanes_of(part, cols)
                copies[chain, 2 * count - 1 - stage].wait_recv()
                if stage > 0:
                    send_up(chain, stage - 1)
                other = start_of(orders[part][:stage])
                other = other + (1 - bit_of(orders[part][stage])) * size
                place = pl.ds(pl.multiple_of(other, size), size)
                sums[w, :, lanes] += square_sum(blocks[w, place, lanes].astype(F32))
        for copy in copies.values():
            copy.wait_send()
        scales = [
            norms[w] / jnp.sqrt(jnp.sum(sums[w], keepdims=True) + 1e-06)
            for w in range(GROUP)
        ]

    w_swap.wait()
    w_share = pltpu.make_async_remote_copy(
        src_ref=w_far.at[own_rows, :],
        dst_ref=w_far.at[own_rows, :],
        send_sem=share_sem.at[0],
        recv_sem=share_sem.at[1],
        device_id=partner(0),
        device_id_type=MESH,
    )
    w_share.start()
    o_swaps = []
    for t in range(4):
        at = slice(t * tile, (t + 1) * tile)
        act = dot(q[at, :], blocks[0]) * scales[0]
        lin = dot(q[at, :], blocks[1]) * scales[1]
        hidq = (act * jax.nn.sigmoid(act) * lin).astype(BF16)
        piece = dot(hidq, blocks[2], ((1,), (1,))) * scales[2]
        near[at, :] = piece.astype(BF16)
        o_swap = swap(1 + t, near.at[at, :], far.at[at, :])
        o_swap.start()
        o_swaps.append(o_swap)
    w_copy.wait()
    width = half // 5

    def near_cols_of(c, carry):
        lanes = pl.ds(pl.multiple_of(c * width, 128), width)
        total_out[:, lanes] = dot(near[...], w_near[:, lanes])
        return carry

    lax.fori_loop(0, 5, near_cols_of, 0)
    w_share.wait()
    for t in range(4):
        at = slice(t * tile, (t + 1) * tile)
        o_swaps[t].wait_recv()

        def far_cols_of(c, carry):
            lanes = pl.ds(pl.multiple_of(c * width, 128), width)
            added = total_out[at, lanes] + dot(far[at, :], w_far[:, lanes])
            out[at, lanes] = added.astype(BF16)
            return carry

        lax.fori_loop(0, 5, far_cols_of, 0)
    for o_swap in o_swaps:
        o_swap.wait_send()


def shards(n_ctx, queries, keys, values, rates, w_up, w_gate, w_down, w_out):
    tokens, rows = keys.shape
    cols = w_up.shape[2]
    half = w_out.shape[1] // 2
    count = n_ctx.bit_length() - 1
    chains = PARTS * GROUP
    vmem = pl.BlockSpec(memory_space=pltpu.VMEM)
    return pl.pallas_call(
        functools.partial(layer_kernel, n_ctx),
        out_shape=jax.ShapeDtypeStruct((tokens, half), BF16),
        in_specs=[vmem] * 7 + [pl.BlockSpec(memory_space=pl.ANY)],
        out_specs=vmem,
        scratch_shapes=[
            pltpu.VMEM((GROUP, rows >> (stage + 1), cols), BF16)
            for stage in range(count)
        ]
        + [
            pltpu.VMEM((GROUP, rows >> (stage + 1), cols), BF16)
            for stage in range(count - 1)
        ]
        + [
            pltpu.VMEM((rows, tokens), BF16),
            pltpu.VMEM((tokens, rows), BF16),
            pltpu.VMEM((rows, tokens), BF16),
            pltpu.VMEM((rows, cols), BF16),
            pltpu.VMEM((GROUP, rows, cols), BF16),
            pltpu.VMEM((GROUP, rows, cols), BF16),
            pltpu.VMEM((GROUP, tokens, cols), BF16),
            pltpu.VMEM((GROUP, rows // n_ctx, cols), F32),
            pltpu.VMEM((GROUP, 8, cols), F32),
            pltpu.VMEM((rows, half), BF16),
            pltpu.VMEM((rows, half), BF16),
            pltpu.VMEM((tokens, rows), BF16),
            pltpu.VMEM((tokens, rows), BF16),
            pltpu.VMEM((tokens, half), F32),
            pltpu.SemaphoreType.DMA((chains, 2 * count)),
            pltpu.SemaphoreType.DMA((chains, 2 * count)),
            pltpu.SemaphoreType.DMA((5,)),
            pltpu.SemaphoreType.DMA((5,)),
            pltpu.SemaphoreType.DMA((2,)),
            pltpu.SemaphoreType.DMA,
        ],
        compiler_params=pltpu.CompilerParams(
            collective_id=0, has_side_effects=True, vmem_limit_bytes=60 << 20
        ),
    )(queries, keys, values, rates, w_up[0], w_gate[0], w_down[0], w_out)


def solution(mesh):
    def body(*args):
        return shards(mesh.shape["ctx"], *args)

    return jax.shard_map(
        body,
        mesh=mesh,
        in_specs=(
            P("ctx", "head"),
            P("ctx", "head"),
            P("ctx", "head"),
            P("ctx", "head"),
            P("head", None, None),
            P("head", None, None),
            P("head", None, None),
            P("head", None),
        ),
        out_specs=P("ctx", "head"),
        check_vma=False,
    )
```

```python
import functools

import jax
import jax.numpy as jnp
from jax import lax
from jax.experimental import pallas as pl
from jax.experimental.pallas import tpu as pltpu
from jax.sharding import PartitionSpec as P

STEPS = 2
F32 = jnp.float32
BF16 = jnp.bfloat16
MESH = pl.DeviceIdType.MESH
GROUP = 3


PARTS = 4


def orders_of(n_ctx):
    count = n_ctx.bit_length() - 1
    middle, low, high = list(range(1, count - 2)), count - 2, count - 1
    return [
        [0] + middle + [low, high],
        [0] + middle + [high, low],
        [0, low, high] + middle,
        [0, high, low] + middle,
    ]


def raw_bit(me, bit):
    return (me // (1 << bit)) % 2


def half_of(me, stage, count):
    if stage == count - 2:
        return (raw_bit(me, count - 2) + raw_bit(me, count - 1)) % 2
    return raw_bit(me, stage)


def partner_of(me, stage, count):
    flips = (count - 2, count - 1) if stage == count - 1 else (stage,)
    for bit in flips:
        me = me + (1 - 2 * raw_bit(me, bit)) * (1 << bit)
    return me


def lanes_of(part, cols):
    width = cols // PARTS
    return slice(part * width, (part + 1) * width)


def dot(left, right, dims=((1,), (0,))):
    return lax.dot_general(left, right, (dims, ((), ())), preferred_element_type=F32)


def square_sum(block):
    return jnp.sum((block * block).reshape(-1, 8, block.shape[-1]), axis=0)


def layer_kernel(
    n_ctx, q, k, v, r, w0, w1, w2, w_out, out, *scratch
):
    count = n_ctx.bit_length() - 1
    recvs, scratch = scratch[:count], scratch[count:]
    accs, scratch = scratch[: count - 1], scratch[count - 1 :]
    (
        kt, u, ut, first2, grads, blocks, mid, kept, sums,
        w_near, w_far, near, far, total_out,
        send_sem, recv_sem, swap_send, swap_recv, share_sem, local_sem,
    ) = scratch
    tokens, rows = k.shape
    cols = w0.shape[1]
    half = w_out.shape[1] // 2
    orders = orders_of(n_ctx)
    me = lax.axis_index("ctx")
    head = lax.axis_index("head")

    def bit_of(stage):
        return half_of(me, stage, count)

    def partner(stage):
        return {"ctx": partner_of(me, stage, count)}

    def start_of(order):
        start, left = 0, rows
        for stage in order:
            left = left // 2
            start = start + bit_of(stage) * left
        return start

    across = {"head": 1 - head}
    barrier = pltpu.get_barrier_semaphore()
    for target in [partner(stage) for stage in range(count)] + [across]:
        pl.semaphore_signal(barrier, inc=1, device_id=target, device_id_type=MESH)
    pl.semaphore_wait(barrier, count + 1)

    def swap(slot, source, target):
        return pltpu.make_async_remote_copy(
            src_ref=source,
            dst_ref=target,
            send_sem=swap_send.at[slot],
            recv_sem=swap_recv.at[slot],
            device_id=across,
            device_id_type=MESH,
        )

    near_cols = pl.ds(pl.multiple_of(head * half, 128), half)
    far_cols = pl.ds(pl.multiple_of((1 - head) * half, 128), half)
    depth = rows // 2
    own_rows = pl.ds(pl.multiple_of(raw_bit(me, 0) * depth, depth), depth)
    w_swap = swap(0, w_out.at[own_rows, far_cols], w_far.at[own_rows, :])
    w_swap.start()
    w_copy = pltpu.make_async_copy(w_out.at[:, near_cols], w_near, local_sem)
    w_copy.start()

    tile = tokens // 4
    for t in range(4):
        at = slice(t * tile, (t + 1) * tile)
        scaled = (r[at, :] * v[at, :].astype(F32)).astype(BF16)
        u[at, :] = scaled
        ut[:, at] = scaled.T
        kt[:, at] = k[at, :].T
    for t in range(cols // 128):
        at = slice(t * 128, (t + 1) * 128)
        first2[:, at] = w2[at, :].T

    chains = [(w, part) for w in range(GROUP) for part in range(PARTS)]
    by_part = sorted(enumerate(chains), key=lambda item: item[1][1])
    middle_first = by_part
    ring_first = by_part[PARTS // 2 * GROUP :] + by_part[: PARTS // 2 * GROUP]
    firsts = (w0, w1, first2)
    scales = [None] * GROUP
    for step in range(STEPS):
        now = firsts if step == 0 else [blocks.at[w] for w in range(GROUP)]
        copies = {}

        def scaled_dot(w, left):
            product = dot(left, now[w][...])
            return product if scales[w] is None else product * scales[w]

        for t in range(2):
            at = slice(t * (tokens // 2), (t + 1) * (tokens // 2))
            act = scaled_dot(0, k[at, :])
            lin = scaled_dot(1, k[at, :])
            err = scaled_dot(2, u[at, :])
            sig = jax.nn.sigmoid(act)
            gate = act * sig
            mid[0, at, :] = (err * lin * sig * (1.0 + act * (1.0 - sig))).astype(BF16)
            mid[1, at, :] = (err * gate).astype(BF16)
            mid[2, at, :] = (gate * lin).astype(BF16)

        def send(chain, slot, source, target, bit):
            copy = pltpu.make_async_remote_copy(
                src_ref=source,
                dst_ref=target,
                send_sem=send_sem.at[chain, slot],
                recv_sem=recv_sem.at[chain, slot],
                device_id=partner(bit),
                device_id_type=MESH,
            )
            copy.start()
            copies[chain, slot] = copy

        def send_down(chain, stage):
            w, part = chains[chain]
            lanes = lanes_of(part, cols)
            bit = orders[part][stage]
            size = rows >> (stage + 1)
            away = pl.ds(pl.multiple_of((1 - bit_of(bit)) * size, size), size)
            origin = grads if stage == 0 else accs[stage - 1]
            source = origin.at[w, away, lanes]
            send(chain, stage, source, recvs[stage].at[w, :, lanes], bit)

        def region(chain, stage):
            w, part = chains[chain]
            size = rows >> stage
            start = start_of(orders[part][:stage])
            return pl.ds(pl.multiple_of(start, size), size)

        def send_up(chain, stage):
            w, part = chains[chain]
            place = blocks.at[w, region(chain, stage + 1), lanes_of(part, cols)]
            send(chain, 2 * count - 1 - stage, place, place, orders[part][stage])

        for w in range(GROUP):
            left = ut if w == 2 else kt

            def grad_rows(piece, carry):
                at = pl.ds(pl.multiple_of(piece * (rows // 4), rows // 4), rows // 4)
                grads[w, at, :] = dot(left[at, :], mid[w]).astype(BF16)
                return carry

            lax.fori_loop(0, 4, grad_rows, 0)
            for part in range(PARTS):
                send_down(PARTS * w + part, 0)
        if step == 0:
            norms = [
                jnp.sqrt(jnp.sum(square_sum(b[...].astype(F32)), keepdims=True))
                for b in firsts
            ]
        for stage in range(count):
            size = rows >> (stage + 1)
            for chain, (w, part) in ring_first if stage else list(enumerate(chains)):
                lanes = lanes_of(part, cols)
                bit = orders[part][stage]
                close = pl.ds(pl.multiple_of(bit_of(bit) * size, size), size)
                copies[chain, stage].wait_recv()
                origin = grads if stage == 0 else accs[stage - 1]
                held = origin[w, close, lanes].astype(F32)
                total = held + recvs[stage][w, :, lanes].astype(F32)
                if stage < count - 1:
                    accs[stage][w, :, lanes] = total.astype(BF16)
                    send_down(chain, stage + 1)
                else:
                    place = region(chain, count)
                    if step == 0:
                        moved = firsts[w][place, lanes].astype(F32) + total
                    else:
                        moved = kept[w, :, lanes] * scales[w] + total
                    kept[w, :, lanes] = moved
                    rounded = moved.astype(BF16)
                    blocks[w, place, lanes] = rounded
                    send_up(chain, count - 1)
                    sums[w, :, lanes] = square_sum(rounded.astype(F32))
        for stage in reversed(range(count)):
            size = rows >> (stage + 1)
            for chain, (w, part) in middle_first if stage > 1 else ring_first:
                lanes = lanes_of(part, cols)
                copies[chain, 2 * count - 1 - stage].wait_recv()
                if stage > 0:
                    send_up(chain, stage - 1)
                other = start_of(orders[part][:stage])
                other = other + (1 - bit_of(orders[part][stage])) * size
                place = pl.ds(pl.multiple_of(other, size), size)
                sums[w, :, lanes] += square_sum(blocks[w, place, lanes].astype(F32))
        for copy in copies.values():
            copy.wait_send()
        scales = [
            norms[w] / jnp.sqrt(jnp.sum(sums[w], keepdims=True) + 1e-06)
            for w in range(GROUP)
        ]

    w_swap.wait()
    w_share = pltpu.make_async_remote_copy(
        src_ref=w_far.at[own_rows, :],
        dst_ref=w_far.at[own_rows, :],
        send_sem=share_sem.at[0],
        recv_sem=share_sem.at[1],
        device_id=partner(0),
        device_id_type=MESH,
    )
    w_share.start()
    o_swaps = []
    for t in range(4):
        at = slice(t * tile, (t + 1) * tile)
        act = dot(q[at, :], blocks[0]) * scales[0]
        lin = dot(q[at, :], blocks[1]) * scales[1]
        hidq = (act * jax.nn.sigmoid(act) * lin).astype(BF16)
        piece = dot(hidq, blocks[2], ((1,), (1,))) * scales[2]
        near[at, :] = piece.astype(BF16)
        o_swap = swap(1 + t, near.at[at, :], far.at[at, :])
        o_swap.start()
        o_swaps.append(o_swap)
    w_copy.wait()
    width = half // 5

    def near_cols_of(c, carry):
        lanes = pl.ds(pl.multiple_of(c * width, 128), width)
        total_out[:, lanes] = dot(near[...], w_near[:, lanes])
        return carry

    lax.fori_loop(0, 5, near_cols_of, 0)
    w_share.wait()
    for t in range(4):
        at = slice(t * tile, (t + 1) * tile)
        o_swaps[t].wait_recv()

        def far_cols_of(c, carry):
            lanes = pl.ds(pl.multiple_of(c * width, 128), width)
            added = total_out[at, lanes] + dot(far[at, :], w_far[:, lanes])
            out[at, lanes] = added.astype(BF16)
            return carry

        lax.fori_loop(0, 5, far_cols_of, 0)
    for o_swap in o_swaps:
        o_swap.wait_send()


def shards(n_ctx, queries, keys, values, rates, w_up, w_gate, w_down, w_out):
    tokens, rows = keys.shape
    cols = w_up.shape[2]
    half = w_out.shape[1] // 2
    count = n_ctx.bit_length() - 1
    chains = PARTS * GROUP
    vmem = pl.BlockSpec(memory_space=pltpu.VMEM)
    return pl.pallas_call(
        functools.partial(layer_kernel, n_ctx),
        out_shape=jax.ShapeDtypeStruct((tokens, half), BF16),
        in_specs=[vmem] * 7 + [pl.BlockSpec(memory_space=pl.ANY)],
        out_specs=vmem,
        scratch_shapes=[
            pltpu.VMEM((GROUP, rows >> (stage + 1), cols), BF16)
            for stage in range(count)
        ]
        + [
            pltpu.VMEM((GROUP, rows >> (stage + 1), cols), BF16)
            for stage in range(count - 1)
        ]
        + [
            pltpu.VMEM((rows, tokens), BF16),
            pltpu.VMEM((tokens, rows), BF16),
            pltpu.VMEM((rows, tokens), BF16),
            pltpu.VMEM((rows, cols), BF16),
            pltpu.VMEM((GROUP, rows, cols), BF16),
            pltpu.VMEM((GROUP, rows, cols), BF16),
            pltpu.VMEM((GROUP, tokens, cols), BF16),
            pltpu.VMEM((GROUP, rows // n_ctx, cols), F32),
            pltpu.VMEM((GROUP, 8, cols), F32),
            pltpu.VMEM((rows, half), BF16),
            pltpu.VMEM((rows, half), BF16),
            pltpu.VMEM((tokens, rows), BF16),
            pltpu.VMEM((tokens, rows), BF16),
            pltpu.VMEM((tokens, half), F32),
            pltpu.SemaphoreType.DMA((chains, 2 * count)),
            pltpu.SemaphoreType.DMA((chains, 2 * count)),
            pltpu.SemaphoreType.DMA((5,)),
            pltpu.SemaphoreType.DMA((5,)),
            pltpu.SemaphoreType.DMA((2,)),
            pltpu.SemaphoreType.DMA,
        ],
        compiler_params=pltpu.CompilerParams(
            collective_id=0, has_side_effects=True, vmem_limit_bytes=60 << 20
        ),
    )(queries, keys, values, rates, w_up[0], w_gate[0], w_down[0], w_out)


def solution(mesh):
    def body(*args):
        return shards(mesh.shape["ctx"], *args)

    return jax.shard_map(
        body,
        mesh=mesh,
        in_specs=(
            P("ctx", "head"),
            P("ctx", "head"),
            P("ctx", "head"),
            P("ctx", "head"),
            P("head", None, None),
            P("head", None, None),
            P("head", None, None),
            P("head", None),
        ),
        out_specs=P("ctx", "head"),
        check_vma=False,
    )
```
